512 devices in a mesh: pair: 64 (over y, z), intg: 8 (over x, core).
Axes of the slice: x: 4, y: 8, z: 8, core: 2. Of those that a mesh axis runs over, the one named last changes fastest.
Arguments:
- amplitudes: bfloat16 [512, 128, 1024], P('pair'), may hold values from -6 to 6
- integrals: bfloat16 [2048, 128, 1024], P('intg', 'pair'), may hold values from -0.015625 to 0.015625
- tile_irreps: int32 [24], replicated, may hold values from 0 to 1
- screening: int32 [128], replicated, may hold values 0 or 1
- slot_tiles: int32 [128], replicated, may hold values from 0 to 127, each once
- pair_list: int32 [512, 2], P('pair'), may hold values from 0 to 299
- occupied_energy: float32 [300], replicated, may hold values from -1.2 to -0.3
- virtual_energy: float32 [768], replicated, may hold values from 0.2 to 1.5
Outputs:
- update: float32 [512, 2048], P('pair', 'intg')
The draws below stay inside these ranges and needn't reach their ends.
Inputs may be any that keep to these rules, and one draw needn't show every extreme that they name: slot_tiles names every cd tile pair of the slab exactly once.
All inputs are finite; a program needn't handle non-finite values.
Results may differ from the reference program's by a relative error of at most 0.0003.
Values may be sent and summed in bfloat16 or wider, within the bound.
No kernel may reach another device: no remote copies, remote signals or barrier semaphores. Data moves between devices by JAX's collectives and lax.ppermute only.
A program may use at most 64 MiB of HBM per device.

```python
import jax
import jax.numpy as jnp
from jax import lax

TILE = 32
NT = 24
NOCC = 300
NIRREP = 2
AB_DEV = 256
TT = 1024
PAIRS = 512
CDT = 128
ABT = 2048
N_INTG = 8


def set_ends(array, rng, smallest, largest):
    extent = array.shape
    index_at = [jax.random.randint(jax.random.fold_in(rng, axis), (), 0, extent[axis]) for axis in range(len(extent))]
    array = array.at[tuple(index_at)].set(smallest)
    longest = extent.index(max(extent))
    index_at[longest] = (index_at[longest] + 1) % extent[longest]
    return array.at[tuple(index_at)].set(largest)


def steps_of(key, extent, split, least, largest):
    level = 1.0
    for dim, blocks in split:
        heights = jax.random.uniform(jax.random.fold_in(jax.random.fold_in(key, 6), dim), (blocks,), jnp.float32, least / len(split), largest / len(split))
        level = level * jnp.repeat(jnp.exp(heights), extent[dim] // blocks).reshape((-1,) + (1,) * (len(extent) - 1 - dim))
    return level


def centred(own_key, shape, deviation, most, pieces=(), held_as=jnp.bfloat16):
    factor_of = steps_of(own_key, shape, pieces, -0.22, 0.18) if pieces else 1.0
    drawn = jax.random.normal(own_key, shape, jnp.float32) * deviation * factor_of
    return jnp.minimum(jnp.maximum(drawn, -most), most).astype(held_as)


def setup_inputs(seed: int = 0) -> dict:
    key_of = jax.random.split(jax.random.key(seed), 9)
    amplitudes = centred(key_of[0], (PAIRS, CDT, TT), 1.0, 6.0, ((0, 64),))
    integrals = centred(key_of[1], (ABT, CDT, TT), (CDT * TT) ** -0.5, 0.015625, ((0, 8), (1, 64)))
    tile_irreps = set_ends(jax.random.randint(key_of[2], (NT,), 0, NIRREP), jax.random.fold_in(key_of[2], 1), 0, NIRREP - 1).astype(jnp.int32)
    screening = set_ends((jax.random.randint(key_of[3], (CDT,), 0, 4) < 3).astype(jnp.int32), jax.random.fold_in(key_of[3], 1), 0, 1)
    slot_tiles = jax.random.permutation(key_of[4], CDT).astype(jnp.int32)
    pair_list = set_ends(jax.random.randint(key_of[5], (PAIRS, 2), 0, NOCC), jax.random.fold_in(key_of[5], 1), 0, NOCC - 1).astype(jnp.int32)
    occupied_energy = jnp.clip(jax.random.uniform(key_of[6], (NOCC,), jnp.float32, -1.2, -0.3), -1.2, -0.3)
    virtual_energy = jnp.clip(jax.random.uniform(key_of[7], (NT * TILE,), jnp.float32, 0.2, 1.5), 0.2, 1.5)
    return {"amplitudes": amplitudes, "integrals": integrals, "tile_irreps": tile_irreps, "screening": screening, "slot_tiles": slot_tiles, "pair_list": pair_list, "occupied_energy": occupied_energy, "virtual_energy": virtual_energy}


def reference(amplitudes, integrals, tile_irreps, screening, slot_tiles, pair_list, occupied_energy, virtual_energy):
    blocks = jnp.arange(N_INTG, dtype=jnp.int32)
    sym_ab = jnp.bitwise_xor(tile_irreps[blocks // NT], tile_irreps[blocks % NT])
    sym_cd = jnp.bitwise_xor(tile_irreps[slot_tiles // NT], tile_irreps[slot_tiles % NT])
    keep = jnp.where(sym_ab[:, None] == sym_cd[None, :], 1.0, 0.0).astype(jnp.float32)
    keep = keep * screening[slot_tiles][None, :].astype(jnp.float32)

    def add_slot(total, slot):
        tile_index = slot_tiles[slot].astype(jnp.int32)
        left = lax.dynamic_index_in_dim(amplitudes, tile_index, 1, False)
        right = lax.dynamic_index_in_dim(integrals, slot, 1, False)
        term = lax.dot_general(left, right, (((1,), (1,)), ((), ())), preferred_element_type=jnp.float32)
        weights = jnp.repeat(lax.dynamic_index_in_dim(keep, slot, 1, False), AB_DEV)
        return total + term * weights[None, :], None

    start = jnp.zeros((PAIRS, ABT), jnp.float32)
    ladder, _ = lax.scan(add_slot, start, jnp.arange(CDT, dtype=jnp.int32))
    rows = jnp.arange(ABT, dtype=jnp.int32)
    block_of = rows // AB_DEV
    inner = rows % AB_DEV
    first = (block_of // NT) * TILE + inner // TILE
    second = (block_of % NT) * TILE + inner % TILE
    occupied_sum = occupied_energy[pair_list[:, 0]] + occupied_energy[pair_list[:, 1]]
    virtual_sum = virtual_energy[first] + virtual_energy[second]
    denom = occupied_sum[:, None] - virtual_sum[None, :]
    return ladder / denom
```

```python
import jax
import jax.numpy as jnp
from jax import lax
from jax.experimental import pallas as pl
from jax.experimental.pallas import tpu as pltpu
from jax.sharding import PartitionSpec as P

TILE = 32
NT = 24
CORES = 2


def lookup(table, index):
    places = jnp.arange(table.shape[0], dtype=jnp.int32)
    return jnp.sum(jnp.where(places[None, :] == index[:, None], table[None, :], 0), axis=1)


def pack_kernel(place, slot_ref, amp_ref, out_ref, rows):
    owners, pairs, _ = rows.shape
    tiles = amp_ref.shape[1]
    slots = slot_ref.shape[1]
    tile_at = lax.broadcasted_iota(jnp.int32, (tiles, slots), 0)
    held = jnp.where(tile_at == slot_ref[...], 1.0, 0.0).astype(jnp.bfloat16)
    owner_at = lax.broadcasted_iota(jnp.int32, (owners, slots), 0)
    slot_at = lax.broadcasted_iota(jnp.int32, (owners, slots), 1)
    mine = jnp.where(slot_at == owner_at * CORES + place[1], 1.0, 0.0).astype(jnp.bfloat16)
    select = lax.dot_general(
        mine, held, (((1,), (1,)), ((), ())), preferred_element_type=jnp.float32
    ).astype(jnp.bfloat16)
    for pair in range(pairs):
        rows[:, pair, :] = jnp.dot(select, amp_ref[pair], preferred_element_type=jnp.float32)
    out_ref[...] = rows[...].astype(jnp.bfloat16)


def pack(place, slot_tiles, amplitudes, owners, width):
    pairs, tiles, _ = amplitudes.shape
    return pl.pallas_call(
        pack_kernel,
        out_shape=jax.ShapeDtypeStruct((owners, pairs, width), jnp.bfloat16),
        grid_spec=pltpu.PrefetchScalarGridSpec(
            num_scalar_prefetch=1,
            grid=(1,),
            in_specs=[
                pl.BlockSpec((1, tiles), lambda k, place: (0, 0)),
                pl.BlockSpec((pairs, tiles, width), lambda k, place: (0, 0, place[0])),
            ],
            out_specs=pl.BlockSpec((owners, pairs, width), lambda k, place: (0, 0, 0)),
            scratch_shapes=[pltpu.VMEM((owners, pairs, width), jnp.float32)],
        ),
        compiler_params=pltpu.CompilerParams(vmem_limit_bytes=16 << 20),
        name="pack",
    )(place, slot_tiles[None, :], amplitudes)


def ladder_kernel(place, own_ref, other_ref, mine_ref, theirs_ref, out_ref):
    contract = (((1,), (1,)), ((), ()))
    term = lax.dot_general(
        own_ref[0], mine_ref[0], contract, preferred_element_type=jnp.float32
    ) + lax.dot_general(
        other_ref[0], theirs_ref[0], contract, preferred_element_type=jnp.float32
    )

    @pl.when(pl.program_id(0) == 0)
    def _():
        out_ref[...] = term

    @pl.when(pl.program_id(0) > 0)
    def _():
        out_ref[...] += term


def ladder_sums(place, own, other, ints):
    quarters, rows, width = own.shape
    cols = ints.shape[1]
    return pl.pallas_call(
        ladder_kernel,
        out_shape=jax.ShapeDtypeStruct((rows, cols), jnp.float32),
        grid_spec=pltpu.PrefetchScalarGridSpec(
            num_scalar_prefetch=1,
            grid=(quarters,),
            in_specs=[
                pl.BlockSpec((1, rows, width), lambda k, place: (k, 0, 0)),
                pl.BlockSpec((1, rows, width), lambda k, place: (k, 0, 0)),
                pl.BlockSpec((1, cols, width), lambda k, place: (place[1], 0, k)),
                pl.BlockSpec((1, cols, width), lambda k, place: (1 - place[1], 0, k)),
            ],
            out_specs=pl.BlockSpec((rows, cols), lambda k, place: (0, 0)),
        ),
        compiler_params=pltpu.CompilerParams(vmem_limit_bytes=24 << 20),
        name="ladder",
    )(place, own, other, ints, ints)


def on_device(
    amplitudes,
    integrals,
    tile_irreps,
    screening,
    slot_tiles,
    pair_list,
    occupied_energy,
    virtual_energy,
    n_pair,
    n_intg,
):
    pairs = amplitudes.shape[0]
    slots_here = integrals.shape[1]
    ab_rows = integrals.shape[0]
    block = lax.axis_index("intg")
    owner = lax.axis_index("pair")
    quarters = n_intg // CORES
    width = amplitudes.shape[2] // quarters
    place = jnp.stack([block // CORES, block % CORES]).astype(jnp.int32)

    send = pack(place, slot_tiles, amplitudes, n_pair, width)
    piece = lax.all_to_all(send, "pair", split_axis=0, concat_axis=0, tiled=True)
    piece = piece.reshape(n_pair * pairs, width)

    first_tile = block // NT
    second_tile = block % NT
    sym_ab = jnp.bitwise_xor(
        lookup(tile_irreps, first_tile[None]), lookup(tile_irreps, second_tile[None])
    )
    my_slots = lax.dynamic_slice_in_dim(slot_tiles, owner * slots_here, slots_here)
    sym_cd = jnp.bitwise_xor(
        lookup(tile_irreps, my_slots // NT), lookup(tile_irreps, my_slots % NT)
    )
    keep = jnp.where(sym_cd == sym_ab, 1.0, 0.0).astype(jnp.float32) * lookup(
        screening, my_slots
    ).astype(jnp.float32)
    masked_ints = jnp.transpose(integrals * keep.astype(jnp.bfloat16)[None, :, None], (1, 0, 2))

    same_core = [list(range(core, n_intg, CORES)) for core in range(CORES)]
    own = lax.all_to_all(
        jnp.broadcast_to(piece[None], (quarters,) + piece.shape),
        "intg",
        split_axis=0,
        concat_axis=0,
        tiled=True,
        axis_index_groups=same_core,
    )
    other = lax.ppermute(own, "intg", [(i, i ^ 1) for i in range(n_intg)])
    partial = ladder_sums(place, own, other, masked_ints)
    parts = lax.all_to_all(
        partial.reshape(n_pair, pairs, ab_rows), "pair", split_axis=0, concat_axis=0, tiled=True
    )
    ladder = jnp.sum(parts, axis=0)

    occupied_sum = lookup(occupied_energy, pair_list[:, 0]) + lookup(
        occupied_energy, pair_list[:, 1]
    )
    first_energy = lax.dynamic_slice_in_dim(virtual_energy, first_tile * TILE, TILE)
    second_energy = lax.dynamic_slice_in_dim(virtual_energy, second_tile * TILE, TILE)
    virtual_sum = jnp.repeat(first_energy[: ab_rows // TILE], TILE) + jnp.tile(
        second_energy, ab_rows // TILE
    )
    denom = occupied_sum[:, None] - virtual_sum[None, :]
    return ladder / denom


def solution(mesh):
    placed = (
        P("pair", None, None),
        P("intg", "pair", None),
        P(),
        P(),
        P(),
        P("pair", None),
        P(),
        P(),
    )
    n_pair, n_intg = mesh.shape["pair"], mesh.shape["intg"]

    def part(*arrays):
        return on_device(*arrays, n_pair, n_intg)

    return jax.shard_map(
        part, mesh=mesh, in_specs=placed, out_specs=P("pair", "intg"), check_vma=False
    )
```

```python
import functools

import jax
import jax.numpy as jnp
from jax import lax
from jax.experimental import pallas as pl
from jax.experimental.pallas import tpu as pltpu
from jax.sharding import PartitionSpec as P

TILE = 32
NT = 24
CORES = 2
SLOTS = 2


def lookup(table, index):
    places = jnp.arange(table.shape[0], dtype=jnp.int32)
    return jnp.sum(jnp.where(places[None, :] == index[:, None], table[None, :], 0), axis=1)


def pack_kernel(slot_ref, amp_ref, out_ref, slots_in, amp_in, rows, slot_sem, amp_sems):
    owners, _, width = rows.shape
    steps, half, tiles, _ = amp_in.shape
    slots = slots_in.shape[1]
    core = lax.axis_index("intg") % CORES
    slot_copy = pltpu.make_async_copy(slot_ref, slots_in, slot_sem)
    slot_copy.start()
    amp_copies = [
        pltpu.make_async_copy(
            amp_ref.at[pl.ds(core * half, half), :, pl.ds(step * width, width)],
            amp_in.at[step],
            amp_sems.at[step],
        )
        for step in range(steps)
    ]
    for copy in amp_copies:
        copy.start()
    tile_at = lax.broadcasted_iota(jnp.int32, (tiles, slots), 0)
    owner_at = lax.broadcasted_iota(jnp.int32, (owners, slots), 0)
    slot_at = lax.broadcasted_iota(jnp.int32, (owners, slots), 1)
    slot_copy.wait()
    held = jnp.where(tile_at == slots_in[...], 1.0, 0.0).astype(jnp.bfloat16)
    select = []
    for slot in range(SLOTS):
        mine = jnp.where(slot_at == owner_at * SLOTS + slot, 1.0, 0.0).astype(jnp.bfloat16)
        select.append(
            lax.dot_general(
                mine, held, (((1,), (1,)), ((), ())), preferred_element_type=jnp.float32
            ).astype(jnp.bfloat16)
        )
    select = jnp.concatenate(select)
    for step, copy in enumerate(amp_copies):
        copy.wait()
        for j in range(half):
            picked = jnp.dot(select, amp_in[step, j], preferred_element_type=jnp.float32)
            for slot in range(SLOTS):
                rows[:, slot * half + j, :] = picked[slot * owners : (slot + 1) * owners]
        out_ref[:, :, step * width : (step + 1) * width] = rows[...].astype(jnp.bfloat16)


def pack(slot_tiles, amplitudes, owners):
    pairs, tiles, entries = amplitudes.shape
    half = pairs // CORES
    width = min(256, entries)
    steps = entries // width
    return pl.pallas_call(
        pack_kernel,
        out_shape=jax.ShapeDtypeStruct((owners, SLOTS * half, entries), jnp.bfloat16),
        in_specs=[pl.BlockSpec(memory_space=pltpu.HBM)] * 2,
        out_specs=pl.BlockSpec(memory_space=pltpu.VMEM),
        scratch_shapes=[
            pltpu.VMEM((1, slot_tiles.shape[0]), jnp.int32),
            pltpu.VMEM((steps, half, tiles, width), jnp.bfloat16),
            pltpu.VMEM((owners, SLOTS * half, width), jnp.float32),
            pltpu.SemaphoreType.DMA,
            pltpu.SemaphoreType.DMA((steps,)),
        ],
        compiler_params=pltpu.CompilerParams(vmem_limit_bytes=16 << 20),
        name="pack",
    )(
        pltpu.with_memory_space_constraint(slot_tiles[None, :], pltpu.HBM),
        pltpu.with_memory_space_constraint(amplitudes, pltpu.HBM),
    )


def ladder_kernel(half, mine_ref, theirs_ref, columns_ref, out_ref):
    columns = columns_ref[...]

    def product(ints_ref, slot):
        return lax.dot_general(
            columns,
            ints_ref[slot],
            (((1,), (1,)), ((), ())),
            preferred_element_type=jnp.float32,
        ).reshape(out_ref.shape)

    first = lax.broadcasted_iota(jnp.int32, out_ref.shape, 1) < half
    kept = jnp.where(first, product(mine_ref, 0), product(theirs_ref, 1))
    moved = jnp.where(first, product(theirs_ref, 0), product(mine_ref, 1))
    out_ref[...] = kept + pltpu.roll(moved, half, 1)


def ladder_sums(owners, half, mine, theirs, columns):
    cols = mine.shape[1]
    return pl.pallas_call(
        functools.partial(ladder_kernel, half),
        out_shape=jax.ShapeDtypeStruct((owners, CORES * half, cols), jnp.float32),
        in_specs=[pl.BlockSpec(memory_space=pltpu.VMEM)] * 3,
        out_specs=pl.BlockSpec(memory_space=pltpu.VMEM),
        compiler_params=pltpu.CompilerParams(vmem_limit_bytes=24 << 20),
        name="ladder",
    )(mine, theirs, columns)


def on_device(
    amplitudes,
    integrals,
    tile_irreps,
    screening,
    slot_tiles,
    pair_list,
    occupied_energy,
    virtual_energy,
    n_pair,
    n_intg,
):
    pairs = amplitudes.shape[0]
    slots_here = integrals.shape[1]
    ab_rows = integrals.shape[0]
    block = lax.axis_index("intg")
    owner = lax.axis_index("pair")
    half = pairs // CORES
    swap = [(i, i ^ 1) for i in range(n_intg)]

    send, integrals = lax.optimization_barrier(
        (pack(slot_tiles, amplitudes, n_pair), integrals)
    )
    columns = lax.all_to_all(send, "pair", split_axis=0, concat_axis=0, tiled=True)
    columns = columns.reshape(n_pair * SLOTS * half, amplitudes.shape[2])

    first_tile = block // NT
    second_tile = block % NT
    sym_ab = jnp.bitwise_xor(
        lookup(tile_irreps, first_tile[None]), lookup(tile_irreps, second_tile[None])
    )
    my_slots = lax.dynamic_slice_in_dim(slot_tiles, owner * slots_here, slots_here)
    sym_cd = jnp.bitwise_xor(
        lookup(tile_irreps, my_slots // NT), lookup(tile_irreps, my_slots % NT)
    )
    keep = jnp.where(sym_cd == sym_ab, 1.0, 0.0).astype(jnp.float32) * lookup(
        screening, my_slots
    ).astype(jnp.float32)
    masked_ints = jnp.transpose(integrals * keep.astype(jnp.bfloat16)[None, :, None], (1, 0, 2))

    other_ints = lax.ppermute(masked_ints, "intg", swap)
    partial = ladder_sums(n_pair, half, masked_ints, other_ints, columns)
    parts = lax.all_to_all(partial, "pair", split_axis=0, concat_axis=0, tiled=True)
    halves = jnp.sum(parts, axis=0)
    kept = halves[:half]
    came = lax.ppermute(halves[half:], "intg", swap)
    ladder = jnp.where(
        block % CORES == 0, jnp.concatenate([kept, came]), jnp.concatenate([came, kept])
    )

    occupied_sum = lookup(occupied_energy, pair_list[:, 0]) + lookup(
        occupied_energy, pair_list[:, 1]
    )
    first_energy = lax.dynamic_slice_in_dim(virtual_energy, first_tile * TILE, TILE)
    second_energy = lax.dynamic_slice_in_dim(virtual_energy, second_tile * TILE, TILE)
    virtual_sum = jnp.repeat(first_energy[: ab_rows // TILE], TILE) + jnp.tile(
        second_energy, ab_rows // TILE
    )
    denom = occupied_sum[:, None] - virtual_sum[None, :]
    return ladder / denom


def solution(mesh):
    placed = (
        P("pair", None, None),
        P("intg", "pair", None),
        P(),
        P(),
        P(),
        P("pair", None),
        P(),
        P(),
    )
    n_pair, n_intg = mesh.shape["pair"], mesh.shape["intg"]

    def part(*arrays):
        return on_device(*arrays, n_pair, n_intg)

    return jax.shard_map(
        part, mesh=mesh, in_specs=placed, out_specs=P("pair", "intg"), check_vma=False
    )
```

```python
import functools

import jax
import jax.numpy as jnp
from jax import lax
from jax.experimental import pallas as pl
from jax.experimental.pallas import tpu as pltpu
from jax.sharding import PartitionSpec as P

TILE = 32
NT = 24
CORES = 2
SLOTS = 2
SHARES = 2


def lookup(table, index):
    places = jnp.arange(table.shape[0], dtype=jnp.int32)
    return jnp.sum(jnp.where(places[None, :] == index[:, None], table[None, :], 0), axis=1)


def pack_kernel(slot_ref, amp_ref, out_ref, slots_in, amp_in, rows, slot_sem, amp_sem):
    owners, _, width = rows.shape
    half, tiles, _ = amp_in.shape
    slots = slots_in.shape[1]
    place = lax.axis_index("intg")
    share, core = place // CORES % SHARES, place % CORES
    slot_copy = pltpu.make_async_copy(slot_ref, slots_in, slot_sem)
    amp_copy = pltpu.make_async_copy(
        amp_ref.at[
            pl.ds(core * half, half), :, pl.ds(pl.multiple_of(share * width, width), width)
        ],
        amp_in,
        amp_sem,
    )
    slot_copy.start()
    amp_copy.start()
    tile_at = lax.broadcasted_iota(jnp.int32, (tiles, slots), 0)
    owner_at = lax.broadcasted_iota(jnp.int32, (owners, slots), 0)
    slot_at = lax.broadcasted_iota(jnp.int32, (owners, slots), 1)
    slot_copy.wait()
    held = jnp.where(tile_at == slots_in[...], 1.0, 0.0).astype(jnp.bfloat16)
    select = []
    for slot in range(SLOTS):
        mine = jnp.where(slot_at == owner_at * SLOTS + slot, 1.0, 0.0).astype(jnp.bfloat16)
        select.append(
            lax.dot_general(
                mine, held, (((1,), (1,)), ((), ())), preferred_element_type=jnp.float32
            ).astype(jnp.bfloat16)
        )
    select = jnp.concatenate(select)
    amp_copy.wait()
    for j in range(half):
        picked = jnp.dot(select, amp_in[j], preferred_element_type=jnp.float32)
        for slot in range(SLOTS):
            rows[:, slot * half + j, :] = picked[slot * owners : (slot + 1) * owners]
    out_ref[...] = rows[...].astype(jnp.bfloat16)


def pack(slot_tiles, amplitudes, owners, width):
    pairs, tiles, _ = amplitudes.shape
    half = pairs // CORES
    return pl.pallas_call(
        pack_kernel,
        out_shape=jax.ShapeDtypeStruct((owners, SLOTS * half, width), jnp.bfloat16),
        in_specs=[pl.BlockSpec(memory_space=pltpu.HBM)] * 2,
        out_specs=pl.BlockSpec(memory_space=pltpu.VMEM),
        scratch_shapes=[
            pltpu.VMEM((1, slot_tiles.shape[0]), jnp.int32),
            pltpu.VMEM((half, tiles, width), jnp.bfloat16),
            pltpu.VMEM((owners, SLOTS * half, width), jnp.float32),
            pltpu.SemaphoreType.DMA,
            pltpu.SemaphoreType.DMA,
        ],
        compiler_params=pltpu.CompilerParams(vmem_limit_bytes=16 << 20),
        name="pack",
    )(
        pltpu.with_memory_space_constraint(slot_tiles[None, :], pltpu.HBM),
        pltpu.with_memory_space_constraint(amplitudes, pltpu.HBM),
    )


def ladder_kernel(half, mine_ref, theirs_ref, piece_ref, other_ref, out_ref):
    width = piece_ref.shape[1]
    share = lax.axis_index("intg") // CORES % SHARES
    here = pl.ds(pl.multiple_of(share * width, width), width)
    there = pl.ds(pl.multiple_of((1 - share) * width, width), width)

    def dot(rows, ints):
        return lax.dot_general(
            rows, ints, (((1,), (1,)), ((), ())), preferred_element_type=jnp.float32
        )

    def product(ints_ref, slot):
        total = dot(piece_ref[...], ints_ref[slot, :, here]) + dot(
            other_ref[...], ints_ref[slot, :, there]
        )
        return total.reshape(out_ref.shape)

    first = lax.broadcasted_iota(jnp.int32, out_ref.shape, 1) < half
    kept = jnp.where(first, product(mine_ref, 0), product(theirs_ref, 1))
    moved = jnp.where(first, product(theirs_ref, 0), product(mine_ref, 1))
    out_ref[...] = kept + pltpu.roll(moved, half, 1)


def ladder_sums(owners, half, mine, theirs, piece, other):
    cols = mine.shape[1]
    return pl.pallas_call(
        functools.partial(ladder_kernel, half),
        out_shape=jax.ShapeDtypeStruct((owners, CORES * half, cols), jnp.float32),
        in_specs=[pl.BlockSpec(memory_space=pltpu.VMEM)] * 4,
        out_specs=pl.BlockSpec(memory_space=pltpu.VMEM),
        compiler_params=pltpu.CompilerParams(vmem_limit_bytes=24 << 20),
        name="ladder",
    )(mine, theirs, piece, other)


def on_device(
    amplitudes,
    integrals,
    tile_irreps,
    screening,
    slot_tiles,
    pair_list,
    occupied_energy,
    virtual_energy,
    n_pair,
    n_intg,
):
    pairs = amplitudes.shape[0]
    slots_here = integrals.shape[1]
    ab_rows = integrals.shape[0]
    block = lax.axis_index("intg")
    owner = lax.axis_index("pair")
    width = amplitudes.shape[2] // SHARES

    send, integrals = lax.optimization_barrier(
        (pack(slot_tiles, amplitudes, n_pair, width), integrals)
    )
    piece = lax.all_to_all(send, "pair", split_axis=0, concat_axis=0, tiled=True)
    piece = piece.reshape(n_pair * pairs, width)

    first_tile = block // NT
    second_tile = block % NT
    sym_ab = jnp.bitwise_xor(
        lookup(tile_irreps, first_tile[None]), lookup(tile_irreps, second_tile[None])
    )
    my_slots = lax.dynamic_slice_in_dim(slot_tiles, owner * slots_here, slots_here)
    sym_cd = jnp.bitwise_xor(
        lookup(tile_irreps, my_slots // NT), lookup(tile_irreps, my_slots % NT)
    )
    keep = jnp.where(sym_cd == sym_ab, 1.0, 0.0).astype(jnp.float32) * lookup(
        screening, my_slots
    ).astype(jnp.float32)
    masked_ints = jnp.transpose(integrals * keep.astype(jnp.bfloat16)[None, :, None], (1, 0, 2))

    swap = [(i, i ^ 1) for i in range(n_intg)]
    other_ints = lax.ppermute(masked_ints, "intg", swap)

    ring = [(i, (i + (CORES if i % CORES == 0 else -CORES)) % n_intg) for i in range(n_intg)]
    other = lax.ppermute(piece, "intg", ring)
    half = pairs // CORES
    partial = ladder_sums(n_pair, half, masked_ints, other_ints, piece, other)
    parts = lax.all_to_all(partial, "pair", split_axis=0, concat_axis=0, tiled=True)
    halves = jnp.sum(parts, axis=0)
    kept = halves[:half]
    came = lax.ppermute(halves[half:], "intg", swap)
    ladder = jnp.where(
        block % CORES == 0, jnp.concatenate([kept, came]), jnp.concatenate([came, kept])
    )

    occupied_sum = lookup(occupied_energy, pair_list[:, 0]) + lookup(
        occupied_energy, pair_list[:, 1]
    )
    first_energy = lax.dynamic_slice_in_dim(virtual_energy, first_tile * TILE, TILE)
    second_energy = lax.dynamic_slice_in_dim(virtual_energy, second_tile * TILE, TILE)
    virtual_sum = jnp.repeat(first_energy[: ab_rows // TILE], TILE) + jnp.tile(
        second_energy, ab_rows // TILE
    )
    denom = occupied_sum[:, None] - virtual_sum[None, :]
    return ladder / denom


def solution(mesh):
    placed = (
        P("pair", None, None),
        P("intg", "pair", None),
        P(),
        P(),
        P(),
        P("pair", None),
        P(),
        P(),
    )
    n_pair, n_intg = mesh.shape["pair"], mesh.shape["intg"]

    def part(*arrays):
        return on_device(*arrays, n_pair, n_intg)

    return jax.shard_map(
        part, mesh=mesh, in_specs=placed, out_specs=P("pair", "intg"), check_vma=False
    )
```

```python
import functools

import jax
import jax.numpy as jnp
from jax import lax
from jax.experimental import pallas as pl
from jax.experimental.pallas import tpu as pltpu
from jax.sharding import PartitionSpec as P

TILE = 32
NT = 24
CORES = 2
SLOTS = 2
SHARES = 2


def lookup(table, index):
    places = jnp.arange(table.shape[0], dtype=jnp.int32)
    return jnp.sum(jnp.where(places[None, :] == index[:, None], table[None, :], 0), axis=1)


def owner_in_turn(owners, place):
    return (place + owners // 2 + owners // 16) % owners


def pack_kernel(slot_ref, amp_ref, out_ref, slots_in, amp_in, rows, slot_sem, amp_sem):
    owners, _, width = rows.shape
    half, tiles, _ = amp_in.shape
    slots = slots_in.shape[1]
    place = lax.axis_index("intg")
    share, core = place // CORES % SHARES, place % CORES
    slot_copy = pltpu.make_async_copy(slot_ref, slots_in, slot_sem)
    amp_copy = pltpu.make_async_copy(
        amp_ref.at[
            pl.ds(core * half, half), :, pl.ds(pl.multiple_of(share * width, width), width)
        ],
        amp_in,
        amp_sem,
    )
    slot_copy.start()
    amp_copy.start()
    tile_at = lax.broadcasted_iota(jnp.int32, (tiles, slots), 0)
    owner_at = owner_in_turn(owners, lax.broadcasted_iota(jnp.int32, (owners, slots), 0))
    slot_at = lax.broadcasted_iota(jnp.int32, (owners, slots), 1)
    slot_copy.wait()
    held = jnp.where(tile_at == slots_in[...], 1.0, 0.0).astype(jnp.bfloat16)
    select = []
    for slot in range(SLOTS):
        mine = jnp.where(slot_at == owner_at * SLOTS + slot, 1.0, 0.0).astype(jnp.bfloat16)
        select.append(
            lax.dot_general(
                mine, held, (((1,), (1,)), ((), ())), preferred_element_type=jnp.float32
            ).astype(jnp.bfloat16)
        )
    select = jnp.concatenate(select)
    amp_copy.wait()
    for j in range(half):
        picked = jnp.dot(select, amp_in[j], preferred_element_type=jnp.float32)
        for slot in range(SLOTS):
            rows[:, slot * half + j, :] = picked[slot * owners : (slot + 1) * owners]
    out_ref[...] = rows[...].astype(jnp.bfloat16)


def pack(slot_tiles, amplitudes, owners, width):
    pairs, tiles, _ = amplitudes.shape
    half = pairs // CORES
    return pl.pallas_call(
        pack_kernel,
        out_shape=jax.ShapeDtypeStruct((owners, SLOTS * half, width), jnp.bfloat16),
        in_specs=[pl.BlockSpec(memory_space=pltpu.HBM)] * 2,
        out_specs=pl.BlockSpec(memory_space=pltpu.VMEM),
        scratch_shapes=[
            pltpu.VMEM((1, slot_tiles.shape[0]), jnp.int32),
            pltpu.VMEM((half, tiles, width), jnp.bfloat16),
            pltpu.VMEM((owners, SLOTS * half, width), jnp.float32),
            pltpu.SemaphoreType.DMA,
            pltpu.SemaphoreType.DMA,
        ],
        compiler_params=pltpu.CompilerParams(vmem_limit_bytes=16 << 20),
        name="pack",
    )(
        pltpu.with_memory_space_constraint(slot_tiles[None, :], pltpu.HBM),
        pltpu.with_memory_space_constraint(amplitudes, pltpu.HBM),
    )


def ladder_kernel(half, mine_ref, theirs_ref, piece_ref, other_ref, out_ref):
    width = piece_ref.shape[1]
    share = lax.axis_index("intg") // CORES % SHARES
    here = pl.ds(pl.multiple_of(share * width, width), width)
    there = pl.ds(pl.multiple_of((1 - share) * width, width), width)

    def dot(rows, ints):
        return lax.dot_general(
            rows, ints, (((1,), (1,)), ((), ())), preferred_element_type=jnp.float32
        )

    def product(ints_ref, slot):
        total = dot(piece_ref[...], ints_ref[slot, :, here]) + dot(
            other_ref[...], ints_ref[slot, :, there]
        )
        return total.reshape(out_ref.shape)

    first = lax.broadcasted_iota(jnp.int32, out_ref.shape, 1) < half
    kept = jnp.where(first, product(mine_ref, 0), product(theirs_ref, 1))
    moved = jnp.where(first, product(theirs_ref, 0), product(mine_ref, 1))
    out_ref[...] = kept + pltpu.roll(moved, half, 1)


def ladder_sums(owners, half, mine, theirs, piece, other):
    cols = mine.shape[1]
    return pl.pallas_call(
        functools.partial(ladder_kernel, half),
        out_shape=jax.ShapeDtypeStruct((owners, CORES * half, cols), jnp.float32),
        in_specs=[pl.BlockSpec(memory_space=pltpu.VMEM)] * 4,
        out_specs=pl.BlockSpec(memory_space=pltpu.VMEM),
        compiler_params=pltpu.CompilerParams(vmem_limit_bytes=24 << 20),
        name="ladder",
    )(mine, theirs, piece, other)


def on_device(
    amplitudes,
    integrals,
    tile_irreps,
    screening,
    slot_tiles,
    pair_list,
    occupied_energy,
    virtual_energy,
    n_pair,
    n_intg,
):
    pairs = amplitudes.shape[0]
    slots_here = integrals.shape[1]
    ab_rows = integrals.shape[0]
    block = lax.axis_index("intg")
    owner = lax.axis_index("pair")
    width = amplitudes.shape[2] // SHARES

    in_turn = [[owner_in_turn(n_pair, place) for place in range(n_pair)]]
    send, integrals = lax.optimization_barrier(
        (pack(slot_tiles, amplitudes, n_pair, width), integrals)
    )
    piece = lax.all_to_all(send, "pair", split_axis=0, concat_axis=0, tiled=True, axis_index_groups=in_turn)
    piece = piece.reshape(n_pair * pairs, width)

    first_tile = block // NT
    second_tile = block % NT
    sym_ab = jnp.bitwise_xor(
        lookup(tile_irreps, first_tile[None]), lookup(tile_irreps, second_tile[None])
    )
    my_slots = lax.dynamic_slice_in_dim(slot_tiles, owner * slots_here, slots_here)
    sym_cd = jnp.bitwise_xor(
        lookup(tile_irreps, my_slots // NT), lookup(tile_irreps, my_slots % NT)
    )
    keep = jnp.where(sym_cd == sym_ab, 1.0, 0.0).astype(jnp.float32) * lookup(
        screening, my_slots
    ).astype(jnp.float32)
    masked_ints = jnp.transpose(integrals * keep.astype(jnp.bfloat16)[None, :, None], (1, 0, 2))

    swap = [(i, i ^ 1) for i in range(n_intg)]
    other_ints = lax.ppermute(masked_ints, "intg", swap)

    ring = [(i, (i + (CORES if i % CORES == 0 else -CORES)) % n_intg) for i in range(n_intg)]
    other = lax.ppermute(piece, "intg", ring)
    half = pairs // CORES
    partial = ladder_sums(n_pair, half, masked_ints, other_ints, piece, other)
    parts = lax.all_to_all(partial, "pair", split_axis=0, concat_axis=0, tiled=True, axis_index_groups=in_turn)
    halves = jnp.sum(parts, axis=0)
    kept = halves[:half]
    came = lax.ppermute(halves[half:], "intg", swap)
    ladder = jnp.where(
        block % CORES == 0, jnp.concatenate([kept, came]), jnp.concatenate([came, kept])
    )

    occupied_sum = lookup(occupied_energy, pair_list[:, 0]) + lookup(
        occupied_energy, pair_list[:, 1]
    )
    first_energy = lax.dynamic_slice_in_dim(virtual_energy, first_tile * TILE, TILE)
    second_energy = lax.dynamic_slice_in_dim(virtual_energy, second_tile * TILE, TILE)
    virtual_sum = jnp.repeat(first_energy[: ab_rows // TILE], TILE) + jnp.tile(
        second_energy, ab_rows // TILE
    )
    denom = occupied_sum[:, None] - virtual_sum[None, :]
    return ladder / denom


def solution(mesh):
    placed = (
        P("pair", None, None),
        P("intg", "pair", None),
        P(),
        P(),
        P(),
        P("pair", None),
        P(),
        P(),
    )
    n_pair, n_intg = mesh.shape["pair"], mesh.shape["intg"]

    def part(*arrays):
        return on_device(*arrays, n_pair, n_intg)

    return jax.shard_map(
        part, mesh=mesh, in_specs=placed, out_specs=P("pair", "intg"), check_vma=False
    )
```

```python
import functools

import jax
import jax.numpy as jnp
from jax import lax
from jax.experimental import pallas as pl
from jax.experimental.pallas import tpu as pltpu
from jax.sharding import PartitionSpec as P

TILE = 32
NT = 24
CORES = 2
SLOTS = 2
SHARES = 2


def lookup(table, index):
    places = jnp.arange(table.shape[0], dtype=jnp.int32)
    return jnp.sum(jnp.where(places[None, :] == index[:, None], table[None, :], 0), axis=1)


def owner_in_turn(owners, place):
    return (place + owners // 2 + owners // 16) % owners


def pack_kernel(slot_ref, amp_ref, out_ref, slots_in, amp_in, slot_sem, amp_sem):
    half, tiles, width = amp_in.shape
    slots = slots_in.shape[1]
    owners, per_owner, _ = out_ref.shape
    rows = owners * per_owner
    place = lax.axis_index("intg")
    share, core = place // CORES % SHARES, place % CORES
    slot_copy = pltpu.make_async_copy(slot_ref, slots_in, slot_sem)
    amp_copy = pltpu.make_async_copy(
        amp_ref.at[
            pl.ds(core * half, half), :, pl.ds(pl.multiple_of(share * width, width), width)
        ],
        amp_in,
        amp_sem,
    )
    slot_copy.start()
    amp_copy.start()
    row_at = lax.broadcasted_iota(jnp.int32, (rows, slots), 0)
    slot_at = lax.broadcasted_iota(jnp.int32, (rows, slots), 1)
    owner_at = owner_in_turn(owners, row_at // per_owner)
    wanted = owner_at * SLOTS + row_at // half % SLOTS
    mine = jnp.where(slot_at == wanted, 1.0, 0.0).astype(jnp.bfloat16)
    j_at = lax.broadcasted_iota(jnp.int32, (rows, tiles), 0) % half
    tile_at = lax.broadcasted_iota(jnp.int32, (tiles, slots), 0)
    slot_copy.wait()
    held = jnp.where(tile_at == slots_in[...], 1.0, 0.0).astype(jnp.bfloat16)
    tile_of = lax.dot_general(
        mine, held, (((1,), (1,)), ((), ())), preferred_element_type=jnp.float32
    )
    select = jnp.concatenate(
        [jnp.where(j_at == j, tile_of, 0.0).astype(jnp.bfloat16) for j in range(half)], axis=1
    )
    amp_copy.wait()
    picked = jnp.dot(
        select, amp_in[...].reshape(half * tiles, width), preferred_element_type=jnp.float32
    )
    out_ref[...] = picked.astype(jnp.bfloat16).reshape(out_ref.shape)


def pack(slot_tiles, amplitudes, owners, width):
    pairs, tiles, _ = amplitudes.shape
    half = pairs // CORES
    return pl.pallas_call(
        pack_kernel,
        out_shape=jax.ShapeDtypeStruct((owners, SLOTS * half, width), jnp.bfloat16),
        in_specs=[pl.BlockSpec(memory_space=pltpu.HBM)] * 2,
        out_specs=pl.BlockSpec(memory_space=pltpu.VMEM),
        scratch_shapes=[
            pltpu.VMEM((1, slot_tiles.shape[0]), jnp.int32),
            pltpu.VMEM((half, tiles, width), jnp.bfloat16),
            pltpu.SemaphoreType.DMA,
            pltpu.SemaphoreType.DMA,
        ],
        compiler_params=pltpu.CompilerParams(vmem_limit_bytes=16 << 20),
        name="pack",
    )(
        pltpu.with_memory_space_constraint(slot_tiles[None, :], pltpu.HBM),
        pltpu.with_memory_space_constraint(amplitudes, pltpu.HBM),
    )


def ladder_kernel(half, away, mine_ref, theirs_ref, columns_ref, *refs):
    out_ref = refs[-1]
    width = columns_ref.shape[1]
    share = (lax.axis_index("intg") // CORES + away) % SHARES
    entries = pl.ds(pl.multiple_of(share * width, width), width)

    def product(ints_ref, slot):
        return lax.dot_general(
            columns_ref[...],
            ints_ref[slot, :, entries],
            (((1,), (1,)), ((), ())),
            preferred_element_type=jnp.float32,
        ).reshape(out_ref.shape)

    first = lax.broadcasted_iota(jnp.int32, out_ref.shape, 1) < half
    kept = jnp.where(first, product(mine_ref, 0), product(theirs_ref, 1))
    moved = jnp.where(first, product(theirs_ref, 0), product(mine_ref, 1))
    total = kept + pltpu.roll(moved, half, 1)
    for sum_ref in refs[:-1]:
        total = total + sum_ref[...]
    out_ref[...] = total


def ladder_sums(owners, half, away, *operands):
    cols = operands[0].shape[1]
    return pl.pallas_call(
        functools.partial(ladder_kernel, half, away),
        out_shape=jax.ShapeDtypeStruct((owners, CORES * half, cols), jnp.float32),
        in_specs=[pl.BlockSpec(memory_space=pltpu.VMEM)] * len(operands),
        out_specs=pl.BlockSpec(memory_space=pltpu.VMEM),
        compiler_params=pltpu.CompilerParams(vmem_limit_bytes=24 << 20),
        name="ladder",
    )(*operands)


def on_device(
    amplitudes,
    integrals,
    tile_irreps,
    screening,
    slot_tiles,
    pair_list,
    occupied_energy,
    virtual_energy,
    n_pair,
    n_intg,
):
    pairs = amplitudes.shape[0]
    slots_here = integrals.shape[1]
    ab_rows = integrals.shape[0]
    block = lax.axis_index("intg")
    owner = lax.axis_index("pair")
    width = amplitudes.shape[2] // SHARES

    in_turn = [[owner_in_turn(n_pair, place) for place in range(n_pair)]]
    send, integrals = lax.optimization_barrier(
        (pack(slot_tiles, amplitudes, n_pair, width), integrals)
    )
    piece = lax.all_to_all(send, "pair", split_axis=0, concat_axis=0, tiled=True, axis_index_groups=in_turn)
    piece = piece.reshape(n_pair * pairs, width)

    first_tile = block // NT
    second_tile = block % NT
    sym_ab = jnp.bitwise_xor(
        lookup(tile_irreps, first_tile[None]), lookup(tile_irreps, second_tile[None])
    )
    my_slots = lax.dynamic_slice_in_dim(slot_tiles, owner * slots_here, slots_here)
    sym_cd = jnp.bitwise_xor(
        lookup(tile_irreps, my_slots // NT), lookup(tile_irreps, my_slots % NT)
    )
    keep = jnp.where(sym_cd == sym_ab, 1.0, 0.0).astype(jnp.float32) * lookup(
        screening, my_slots
    ).astype(jnp.float32)
    masked_ints = jnp.transpose(integrals * keep.astype(jnp.bfloat16)[None, :, None], (1, 0, 2))

    swap = [(i, i ^ 1) for i in range(n_intg)]
    other_ints = lax.ppermute(masked_ints, "intg", swap)

    ring = [(i, (i + (CORES if i % CORES == 0 else -CORES)) % n_intg) for i in range(n_intg)]
    other = lax.ppermute(piece, "intg", ring)
    half = pairs // CORES
    partial = ladder_sums(n_pair, half, 0, masked_ints, other_ints, piece)
    partial = ladder_sums(n_pair, half, 1, masked_ints, other_ints, other, partial)
    parts = lax.all_to_all(partial, "pair", split_axis=0, concat_axis=0, tiled=True, axis_index_groups=in_turn)
    halves = jnp.sum(parts, axis=0)
    kept = halves[:half]
    came = lax.ppermute(halves[half:], "intg", swap)
    ladder = jnp.where(
        block % CORES == 0, jnp.concatenate([kept, came]), jnp.concatenate([came, kept])
    )

    occupied_sum = lookup(occupied_energy, pair_list[:, 0]) + lookup(
        occupied_energy, pair_list[:, 1]
    )
    first_energy = lax.dynamic_slice_in_dim(virtual_energy, first_tile * TILE, TILE)
    second_energy = lax.dynamic_slice_in_dim(virtual_energy, second_tile * TILE, TILE)
    virtual_sum = jnp.repeat(first_energy[: ab_rows // TILE], TILE) + jnp.tile(
        second_energy, ab_rows // TILE
    )
    denom = occupied_sum[:, None] - virtual_sum[None, :]
    return ladder / denom


def solution(mesh):
    placed = (
        P("pair", None, None),
        P("intg", "pair", None),
        P(),
        P(),
        P(),
        P("pair", None),
        P(),
        P(),
    )
    n_pair, n_intg = mesh.shape["pair"], mesh.shape["intg"]

    def part(*arrays):
        return on_device(*arrays, n_pair, n_intg)

    return jax.shard_map(
        part, mesh=mesh, in_specs=placed, out_specs=P("pair", "intg"), check_vma=False
    )
```

```python
import functools

import jax
import jax.numpy as jnp
from jax import lax
from jax.experimental import pallas as pl
from jax.experimental.pallas import tpu as pltpu
from jax.sharding import PartitionSpec as P

TILE = 32
NT = 24
CORES = 2
SLOTS = 2
SHARES = 2


def lookup(table, index):
    places = jnp.arange(table.shape[0], dtype=jnp.int32)
    return jnp.sum(jnp.where(places[None, :] == index[:, None], table[None, :], 0), axis=1)


def owner_in_turn(owners, place):
    return (place + owners // 2 + owners // 16) % owners


def pack_kernel(slot_ref, amp_ref, out_ref, slots_in, amp_in, slot_sem, amp_sem):
    half, tiles, width = amp_in.shape
    slots = slots_in.shape[1]
    owners, per_owner, _ = out_ref.shape
    rows = owners * per_owner
    place = lax.axis_index("intg")
    share, core = place // CORES % SHARES, place % CORES
    slot_copy = pltpu.make_async_copy(slot_ref, slots_in, slot_sem)
    amp_copy = pltpu.make_async_copy(
        amp_ref.at[
            pl.ds(core * half, half), :, pl.ds(pl.multiple_of(share * width, width), width)
        ],
        amp_in,
        amp_sem,
    )
    slot_copy.start()
    amp_copy.start()
    row_at = lax.broadcasted_iota(jnp.int32, (rows, slots), 0)
    slot_at = lax.broadcasted_iota(jnp.int32, (rows, slots), 1)
    owner_at = owner_in_turn(owners, row_at // per_owner)
    wanted = owner_at * SLOTS + row_at // half % SLOTS
    mine = jnp.where(slot_at == wanted, 1.0, 0.0).astype(jnp.bfloat16)
    j_at = lax.broadcasted_iota(jnp.int32, (rows, tiles), 0) % half
    tile_at = lax.broadcasted_iota(jnp.int32, (tiles, slots), 0)
    slot_copy.wait()
    held = jnp.where(tile_at == slots_in[...], 1.0, 0.0).astype(jnp.bfloat16)
    tile_of = lax.dot_general(
        mine, held, (((1,), (1,)), ((), ())), preferred_element_type=jnp.float32
    )
    select = jnp.concatenate(
        [jnp.where(j_at == j, tile_of, 0.0).astype(jnp.bfloat16) for j in range(half)], axis=1
    )
    amp_copy.wait()
    picked = jnp.dot(
        select, amp_in[...].reshape(half * tiles, width), preferred_element_type=jnp.float32
    )
    out_ref[...] = picked.astype(jnp.bfloat16).reshape(out_ref.shape)


def pack(slot_tiles, amplitudes, owners, width):
    pairs, tiles, _ = amplitudes.shape
    half = pairs // CORES
    return pl.pallas_call(
        pack_kernel,
        out_shape=jax.ShapeDtypeStruct((owners, SLOTS * half, width), jnp.bfloat16),
        in_specs=[pl.BlockSpec(memory_space=pltpu.HBM)] * 2,
        out_specs=pl.BlockSpec(memory_space=pltpu.VMEM),
        scratch_shapes=[
            pltpu.VMEM((1, slot_tiles.shape[0]), jnp.int32),
            pltpu.VMEM((half, tiles, width), jnp.bfloat16),
            pltpu.SemaphoreType.DMA,
            pltpu.SemaphoreType.DMA,
        ],
        compiler_params=pltpu.CompilerParams(vmem_limit_bytes=16 << 20),
        name="pack",
    )(
        pltpu.with_memory_space_constraint(slot_tiles[None, :], pltpu.HBM),
        pltpu.with_memory_space_constraint(amplitudes, pltpu.HBM),
    )


def ladder_kernel(half, away, mine_ref, theirs_ref, columns_ref, *refs):
    out_ref = refs[-1]
    width = columns_ref.shape[1]
    share = (lax.axis_index("intg") // CORES + away) % SHARES
    entries = pl.ds(pl.multiple_of(share * width, width), width)

    def product(ints_ref, slot):
        return lax.dot_general(
            columns_ref[...],
            ints_ref[slot, :, entries],
            (((1,), (1,)), ((), ())),
            preferred_element_type=jnp.float32,
        ).reshape(out_ref.shape)

    first = lax.broadcasted_iota(jnp.int32, out_ref.shape, 1) < half
    kept = jnp.where(first, product(mine_ref, 0), product(theirs_ref, 1))
    moved = jnp.where(first, product(theirs_ref, 0), product(mine_ref, 1))
    total = kept + pltpu.roll(moved, half, 1)
    for sum_ref in refs[:-1]:
        total = total + sum_ref[...]
    out_ref[...] = total


def ladder_sums(owners, half, away, *operands):
    cols = operands[0].shape[1]
    return pl.pallas_call(
        functools.partial(ladder_kernel, half, away),
        out_shape=jax.ShapeDtypeStruct((owners, CORES * half, cols), jnp.float32),
        in_specs=[pl.BlockSpec(memory_space=pltpu.VMEM)] * len(operands),
        out_specs=pl.BlockSpec(memory_space=pltpu.VMEM),
        compiler_params=pltpu.CompilerParams(vmem_limit_bytes=24 << 20),
        name="ladder",
    )(*operands)


def on_device(
    amplitudes,
    integrals,
    tile_irreps,
    screening,
    slot_tiles,
    pair_list,
    occupied_energy,
    virtual_energy,
    n_pair,
    n_intg,
):
    pairs = amplitudes.shape[0]
    slots_here = integrals.shape[1]
    ab_rows = integrals.shape[0]
    block = lax.axis_index("intg")
    owner = lax.axis_index("pair")
    width = amplitudes.shape[2] // SHARES

    in_turn = [[owner_in_turn(n_pair, place) for place in range(n_pair)]]
    send, integrals = lax.optimization_barrier(
        (pack(slot_tiles, amplitudes, n_pair, width), integrals)
    )
    piece = lax.all_to_all(send, "pair", split_axis=0, concat_axis=0, tiled=True, axis_index_groups=in_turn)
    piece = piece.reshape(n_pair * pairs, width)

    first_tile = block // NT
    second_tile = block % NT
    sym_ab = jnp.bitwise_xor(
        lookup(tile_irreps, first_tile[None]), lookup(tile_irreps, second_tile[None])
    )
    my_slots = lax.dynamic_slice_in_dim(slot_tiles, owner * slots_here, slots_here)
    sym_cd = jnp.bitwise_xor(
        lookup(tile_irreps, my_slots // NT), lookup(tile_irreps, my_slots % NT)
    )
    keep = jnp.where(sym_cd == sym_ab, 1.0, 0.0).astype(jnp.float32) * lookup(
        screening, my_slots
    ).astype(jnp.float32)
    masked_ints = jnp.transpose(integrals * keep.astype(jnp.bfloat16)[None, :, None], (1, 0, 2))

    swap = [(i, i ^ 1) for i in range(n_intg)]
    other_ints = lax.ppermute(masked_ints, "intg", swap)

    ring = [(i, (i + (CORES if i % CORES == 0 else -CORES)) % n_intg) for i in range(n_intg)]
    other = lax.ppermute(piece, "intg", ring)
    half = pairs // CORES
    occupied_sum = lookup(occupied_energy, pair_list[:, 0]) + lookup(
        occupied_energy, pair_list[:, 1]
    )
    first_energy = lax.dynamic_slice_in_dim(virtual_energy, first_tile * TILE, TILE)
    second_energy = lax.dynamic_slice_in_dim(virtual_energy, second_tile * TILE, TILE)
    virtual_sum = jnp.repeat(first_energy[: ab_rows // TILE], TILE) + jnp.tile(
        second_energy, ab_rows // TILE
    )
    denom = occupied_sum[:, None] - virtual_sum[None, :]
    other, denom = lax.optimization_barrier((other, denom))

    partial = ladder_sums(n_pair, half, 0, masked_ints, other_ints, piece)
    partial = ladder_sums(n_pair, half, 1, masked_ints, other_ints, other, partial)
    parts = lax.all_to_all(partial, "pair", split_axis=0, concat_axis=0, tiled=True, axis_index_groups=in_turn)
    halves = jnp.sum(parts, axis=0)
    kept = halves[:half]
    came = lax.ppermute(halves[half:], "intg", swap)
    ladder = jnp.where(
        block % CORES == 0, jnp.concatenate([kept, came]), jnp.concatenate([came, kept])
    )

    return ladder / denom


def solution(mesh):
    placed = (
        P("pair", None, None),
        P("intg", "pair", None),
        P(),
        P(),
        P(),
        P("pair", None),
        P(),
        P(),
    )
    n_pair, n_intg = mesh.shape["pair"], mesh.shape["intg"]

    def part(*arrays):
        return on_device(*arrays, n_pair, n_intg)

    return jax.shard_map(
        part, mesh=mesh, in_specs=placed, out_specs=P("pair", "intg"), check_vma=False
    )
```

```python
import functools

import jax
import jax.numpy as jnp
from jax import lax
from jax.experimental import pallas as pl
from jax.experimental.pallas import tpu as pltpu
from jax.sharding import PartitionSpec as P

TILE = 32
NT = 24
CORES = 2
SLOTS = 2
SHARES = 2


def lookup(table, index):
    places = jnp.arange(table.shape[0], dtype=jnp.int32)
    return jnp.sum(jnp.where(places[None, :] == index[:, None], table[None, :], 0), axis=1)


def owner_in_turn(owners, place):
    return (place + owners // 2 + owners // 16 + 1) % owners


def pack_kernel(slot_ref, amp_ref, out_ref, slots_in, amp_in, slot_sem, amp_sem):
    half, tiles, width = amp_in.shape
    slots = slots_in.shape[1]
    owners, per_owner, _ = out_ref.shape
    rows = owners * per_owner
    place = lax.axis_index("intg")
    share, core = place // CORES % SHARES, place % CORES
    slot_copy = pltpu.make_async_copy(slot_ref, slots_in, slot_sem)
    amp_copy = pltpu.make_async_copy(
        amp_ref.at[
            pl.ds(core * half, half), :, pl.ds(pl.multiple_of(share * width, width), width)
        ],
        amp_in,
        amp_sem,
    )
    slot_copy.start()
    amp_copy.start()
    row_at = lax.broadcasted_iota(jnp.int32, (rows, slots), 0)
    slot_at = lax.broadcasted_iota(jnp.int32, (rows, slots), 1)
    owner_at = owner_in_turn(owners, row_at // per_owner)
    wanted = owner_at * SLOTS + row_at // half % SLOTS
    mine = jnp.where(slot_at == wanted, 1.0, 0.0).astype(jnp.bfloat16)
    j_at = lax.broadcasted_iota(jnp.int32, (rows, tiles), 0) % half
    tile_at = lax.broadcasted_iota(jnp.int32, (tiles, slots), 0)
    slot_copy.wait()
    held = jnp.where(tile_at == slots_in[...], 1.0, 0.0).astype(jnp.bfloat16)
    tile_of = lax.dot_general(
        mine, held, (((1,), (1,)), ((), ())), preferred_element_type=jnp.float32
    )
    select = jnp.concatenate(
        [jnp.where(j_at == j, tile_of, 0.0).astype(jnp.bfloat16) for j in range(half)], axis=1
    )
    amp_copy.wait()
    picked = jnp.dot(
        select, amp_in[...].reshape(half * tiles, width), preferred_element_type=jnp.float32
    )
    out_ref[...] = picked.astype(jnp.bfloat16).reshape(out_ref.shape)


def pack(slot_tiles, amplitudes, owners, width):
    pairs, tiles, _ = amplitudes.shape
    half = pairs // CORES
    return pl.pallas_call(
        pack_kernel,
        out_shape=jax.ShapeDtypeStruct((owners, SLOTS * half, width), jnp.bfloat16),
        in_specs=[pl.BlockSpec(memory_space=pltpu.HBM)] * 2,
        out_specs=pl.BlockSpec(memory_space=pltpu.VMEM),
        scratch_shapes=[
            pltpu.VMEM((1, slot_tiles.shape[0]), jnp.int32),
            pltpu.VMEM((half, tiles, width), jnp.bfloat16),
            pltpu.SemaphoreType.DMA,
            pltpu.SemaphoreType.DMA,
        ],
        compiler_params=pltpu.CompilerParams(vmem_limit_bytes=16 << 20),
        name="pack",
    )(
        pltpu.with_memory_space_constraint(slot_tiles[None, :], pltpu.HBM),
        pltpu.with_memory_space_constraint(amplitudes, pltpu.HBM),
    )


def ladder_kernel(half, away, mine_ref, theirs_ref, columns_ref, *refs):
    out_ref = refs[-1]
    width = columns_ref.shape[1]
    share = (lax.axis_index("intg") // CORES + away) % SHARES
    entries = pl.ds(pl.multiple_of(share * width, width), width)

    def product(ints_ref, slot):
        return lax.dot_general(
            columns_ref[...],
            ints_ref[slot, :, entries],
            (((1,), (1,)), ((), ())),
            preferred_element_type=jnp.float32,
        ).reshape(out_ref.shape)

    first = lax.broadcasted_iota(jnp.int32, out_ref.shape, 1) < half
    kept = jnp.where(first, product(mine_ref, 0), product(theirs_ref, 1))
    moved = jnp.where(first, product(theirs_ref, 0), product(mine_ref, 1))
    total = kept + pltpu.roll(moved, half, 1)
    for sum_ref in refs[:-1]:
        total = total + sum_ref[...]
    out_ref[...] = total


def ladder_sums(owners, half, away, *operands):
    cols = operands[0].shape[1]
    return pl.pallas_call(
        functools.partial(ladder_kernel, half, away),
        out_shape=jax.ShapeDtypeStruct((owners, CORES * half, cols), jnp.float32),
        in_specs=[pl.BlockSpec(memory_space=pltpu.VMEM)] * len(operands),
        out_specs=pl.BlockSpec(memory_space=pltpu.VMEM),
        compiler_params=pltpu.CompilerParams(vmem_limit_bytes=24 << 20),
        name="ladder",
    )(*operands)


def on_device(
    amplitudes,
    integrals,
    tile_irreps,
    screening,
    slot_tiles,
    pair_list,
    occupied_energy,
    virtual_energy,
    n_pair,
    n_intg,
):
    pairs = amplitudes.shape[0]
    slots_here = integrals.shape[1]
    ab_rows = integrals.shape[0]
    block = lax.axis_index("intg")
    owner = lax.axis_index("pair")
    width = amplitudes.shape[2] // SHARES

    in_turn = [[owner_in_turn(n_pair, place) for place in range(n_pair)]]
    send, integrals = lax.optimization_barrier(
        (pack(slot_tiles, amplitudes, n_pair, width), integrals)
    )
    piece = lax.all_to_all(send, "pair", split_axis=0, concat_axis=0, tiled=True, axis_index_groups=in_turn)
    piece = piece.reshape(n_pair * pairs, width)

    first_tile = block // NT
    second_tile = block % NT
    sym_ab = jnp.bitwise_xor(
        lookup(tile_irreps, first_tile[None]), lookup(tile_irreps, second_tile[None])
    )
    my_slots = lax.dynamic_slice_in_dim(slot_tiles, owner * slots_here, slots_here)
    sym_cd = jnp.bitwise_xor(
        lookup(tile_irreps, my_slots // NT), lookup(tile_irreps, my_slots % NT)
    )
    keep = jnp.where(sym_cd == sym_ab, 1.0, 0.0).astype(jnp.float32) * lookup(
        screening, my_slots
    ).astype(jnp.float32)
    masked_ints = jnp.transpose(integrals * keep.astype(jnp.bfloat16)[None, :, None], (1, 0, 2))

    swap = [(i, i ^ 1) for i in range(n_intg)]
    other_ints = lax.ppermute(masked_ints, "intg", swap)

    ring = [(i, (i + (CORES if i % CORES == 0 else -CORES)) % n_intg) for i in range(n_intg)]
    other = lax.ppermute(piece, "intg", ring)
    half = pairs // CORES
    occupied_sum = lookup(occupied_energy, pair_list[:, 0]) + lookup(
        occupied_energy, pair_list[:, 1]
    )
    first_energy = lax.dynamic_slice_in_dim(virtual_energy, first_tile * TILE, TILE)
    second_energy = lax.dynamic_slice_in_dim(virtual_energy, second_tile * TILE, TILE)
    virtual_sum = jnp.repeat(first_energy[: ab_rows // TILE], TILE) + jnp.tile(
        second_energy, ab_rows // TILE
    )
    denom = occupied_sum[:, None] - virtual_sum[None, :]
    other, denom = lax.optimization_barrier((other, denom))

    partial = ladder_sums(n_pair, half, 0, masked_ints, other_ints, piece)
    partial = ladder_sums(n_pair, half, 1, masked_ints, other_ints, other, partial)
    parts = lax.all_to_all(partial, "pair", split_axis=0, concat_axis=0, tiled=True, axis_index_groups=in_turn)
    halves = jnp.sum(parts, axis=0)
    kept = halves[:half]
    came = lax.ppermute(halves[half:], "intg", swap)
    ladder = jnp.where(
        block % CORES == 0, jnp.concatenate([kept, came]), jnp.concatenate([came, kept])
    )

    return ladder / denom


def solution(mesh):
    placed = (
        P("pair", None, None),
        P("intg", "pair", None),
        P(),
        P(),
        P(),
        P("pair", None),
        P(),
        P(),
    )
    n_pair, n_intg = mesh.shape["pair"], mesh.shape["intg"]

    def part(*arrays):
        return on_device(*arrays, n_pair, n_intg)

    return jax.shard_map(
        part, mesh=mesh, in_specs=placed, out_specs=P("pair", "intg"), check_vma=False
    )
```

```python
import functools

import jax
import jax.numpy as jnp
from jax import lax
from jax.experimental import pallas as pl
from jax.experimental.pallas import tpu as pltpu
from jax.sharding import PartitionSpec as P

TILE = 32
NT = 24
CORES = 2
SLOTS = 2
SHARES = 2


def lookup(table, index):
    places = jnp.arange(table.shape[0], dtype=jnp.int32)
    return jnp.sum(jnp.where(places[None, :] == index[:, None], table[None, :], 0), axis=1)


def owner_in_turn(owners, place):
    return (place + owners // 2 + owners // 16 + 1) % owners


def pack_kernel(slot_ref, amp_ref, out_ref, slots_in, amp_in, slot_sem, amp_sem):
    half, tiles, width = amp_in.shape
    slots = slots_in.shape[1]
    owners, per_owner, _ = out_ref.shape
    rows = owners * per_owner
    place = lax.axis_index("intg")
    share, core = place // CORES % SHARES, place % CORES
    slot_copy = pltpu.make_async_copy(slot_ref, slots_in, slot_sem)
    amp_copy = pltpu.make_async_copy(
        amp_ref.at[
            pl.ds(core * half, half), :, pl.ds(pl.multiple_of(share * width, width), width)
        ],
        amp_in,
        amp_sem,
    )
    slot_copy.start()
    amp_copy.start()
    row_at = lax.broadcasted_iota(jnp.int32, (rows, slots), 0)
    slot_at = lax.broadcasted_iota(jnp.int32, (rows, slots), 1)
    owner_at = owner_in_turn(owners, row_at // per_owner)
    wanted = owner_at * SLOTS + row_at // half % SLOTS
    mine = jnp.where(slot_at == wanted, 1.0, 0.0).astype(jnp.bfloat16)
    j_at = lax.broadcasted_iota(jnp.int32, (rows, tiles), 0) % half
    tile_at = lax.broadcasted_iota(jnp.int32, (tiles, slots), 0)
    slot_copy.wait()
    held = jnp.where(tile_at == slots_in[...], 1.0, 0.0).astype(jnp.bfloat16)
    tile_of = lax.dot_general(
        mine, held, (((1,), (1,)), ((), ())), preferred_element_type=jnp.float32
    )
    select = jnp.concatenate(
        [jnp.where(j_at == j, tile_of, 0.0).astype(jnp.bfloat16) for j in range(half)], axis=1
    )
    amp_copy.wait()
    picked = jnp.dot(
        select, amp_in[...].reshape(half * tiles, width), preferred_element_type=jnp.float32
    )
    out_ref[...] = picked.astype(jnp.bfloat16).reshape(out_ref.shape)


def pack(slot_tiles, amplitudes, owners, width):
    pairs, tiles, _ = amplitudes.shape
    half = pairs // CORES
    return pl.pallas_call(
        pack_kernel,
        out_shape=jax.ShapeDtypeStruct((owners, SLOTS * half, width), jnp.bfloat16),
        in_specs=[pl.BlockSpec(memory_space=pltpu.HBM)] * 2,
        out_specs=pl.BlockSpec(memory_space=pltpu.VMEM),
        scratch_shapes=[
            pltpu.VMEM((1, slot_tiles.shape[0]), jnp.int32),
            pltpu.VMEM((half, tiles, width), jnp.bfloat16),
            pltpu.SemaphoreType.DMA,
            pltpu.SemaphoreType.DMA,
        ],
        compiler_params=pltpu.CompilerParams(vmem_limit_bytes=16 << 20),
        name="pack",
    )(
        pltpu.with_memory_space_constraint(slot_tiles[None, :], pltpu.HBM),
        pltpu.with_memory_space_constraint(amplitudes, pltpu.HBM),
    )


def ladder_kernel(half, away, mine_ref, theirs_ref, columns_ref, *refs):
    out_ref = refs[-1]
    width = columns_ref.shape[1]
    share = (lax.axis_index("intg") // CORES + away) % SHARES
    entries = pl.ds(pl.multiple_of(share * width, width), width)

    def product(ints_ref, slot):
        return lax.dot_general(
            columns_ref[...],
            ints_ref[slot, :, entries],
            (((1,), (1,)), ((), ())),
            preferred_element_type=jnp.float32,
        ).reshape(out_ref.shape)

    first = lax.broadcasted_iota(jnp.int32, out_ref.shape, 1) < half
    kept = jnp.where(first, product(mine_ref, 0), product(theirs_ref, 1))
    moved = jnp.where(first, product(theirs_ref, 0), product(mine_ref, 1))
    total = kept + pltpu.roll(moved, half, 1)
    for sum_ref in refs[:-1]:
        total = total + sum_ref[...]
    out_ref[...] = total


def ladder_sums(owners, half, away, *operands):
    cols = operands[0].shape[1]
    return pl.pallas_call(
        functools.partial(ladder_kernel, half, away),
        out_shape=jax.ShapeDtypeStruct((owners, CORES * half, cols), jnp.float32),
        in_specs=[pl.BlockSpec(memory_space=pltpu.VMEM)] * len(operands),
        out_specs=pl.BlockSpec(memory_space=pltpu.VMEM),
        compiler_params=pltpu.CompilerParams(vmem_limit_bytes=24 << 20),
        name="ladder",
    )(*operands)


def on_device(
    amplitudes,
    integrals,
    tile_irreps,
    screening,
    slot_tiles,
    pair_list,
    occupied_energy,
    virtual_energy,
    n_pair,
    n_intg,
):
    pairs = amplitudes.shape[0]
    slots_here = integrals.shape[1]
    ab_rows = integrals.shape[0]
    block = lax.axis_index("intg")
    owner = lax.axis_index("pair")
    width = amplitudes.shape[2] // SHARES

    in_turn = [[owner_in_turn(n_pair, place) for place in range(n_pair)]]
    send, integrals = lax.optimization_barrier(
        (pack(slot_tiles, amplitudes, n_pair, width), integrals)
    )
    piece = lax.all_to_all(send, "pair", split_axis=0, concat_axis=0, tiled=True, axis_index_groups=in_turn)
    piece = piece.reshape(n_pair * pairs, width)

    first_tile = block // NT
    second_tile = block % NT
    sym_ab = jnp.bitwise_xor(
        lookup(tile_irreps, first_tile[None]), lookup(tile_irreps, second_tile[None])
    )
    my_slots = lax.dynamic_slice_in_dim(slot_tiles, owner * slots_here, slots_here)
    sym_cd = jnp.bitwise_xor(
        lookup(tile_irreps, my_slots // NT), lookup(tile_irreps, my_slots % NT)
    )
    keep = jnp.where(sym_cd == sym_ab, 1.0, 0.0).astype(jnp.float32) * lookup(
        screening, my_slots
    ).astype(jnp.float32)
    masked_ints = jnp.transpose(integrals * keep.astype(jnp.bfloat16)[None, :, None], (1, 0, 2))

    swap = [(i, i ^ 1) for i in range(n_intg)]
    other_ints = lax.ppermute(masked_ints, "intg", swap)

    ring = [(i, (i + (CORES if i % CORES == 0 else -CORES)) % n_intg) for i in range(n_intg)]
    other = lax.ppermute(piece, "intg", ring)
    half = pairs // CORES
    occupied_sum = lookup(occupied_energy, pair_list[:, 0]) + lookup(
        occupied_energy, pair_list[:, 1]
    )
    first_energy = lax.dynamic_slice_in_dim(virtual_energy, first_tile * TILE, TILE)
    second_energy = lax.dynamic_slice_in_dim(virtual_energy, second_tile * TILE, TILE)
    virtual_sum = jnp.repeat(first_energy[: ab_rows // TILE], TILE) + jnp.tile(
        second_energy, ab_rows // TILE
    )
    denom = occupied_sum[:, None] - virtual_sum[None, :]
    other, denom = lax.optimization_barrier((other, denom))

    partial = ladder_sums(n_pair, half, 0, masked_ints, other_ints, piece)
    partial = ladder_sums(n_pair, half, 1, masked_ints, other_ints, other, partial)
    parts = lax.all_to_all(partial, "pair", split_axis=0, concat_axis=0, tiled=True, axis_index_groups=in_turn)
    halves = jnp.sum(parts, axis=0)
    kept = halves[:half]
    came = lax.ppermute(halves, "intg", swap)[half:]
    ladder = jnp.where(
        block % CORES == 0, jnp.concatenate([kept, came]), jnp.concatenate([came, kept])
    )

    return ladder / denom


def solution(mesh):
    placed = (
        P("pair", None, None),
        P("intg", "pair", None),
        P(),
        P(),
        P(),
        P("pair", None),
        P(),
        P(),
    )
    n_pair, n_intg = mesh.shape["pair"], mesh.shape["intg"]

    def part(*arrays):
        return on_device(*arrays, n_pair, n_intg)

    return jax.shard_map(
        part, mesh=mesh, in_specs=placed, out_specs=P("pair", "intg"), check_vma=False
    )
```
